32 devices in a mesh: ctx: 4 (over x, core), mod: 2 (over y), seq: 4 (over z).
Axes of the slice: x: 2, y: 2, z: 4, core: 2. Of those that a mesh axis runs over, the one named last changes fastest.
Arguments:
- inputs: bfloat16 [4, 1024, 8192], P('seq', 'ctx', 'mod'), may hold values from -6 to 6
- out_grads: bfloat16 [4, 1024, 28672], P('seq', 'ctx', 'mod'), may hold values from -6 to 6
- proj_in: bfloat16 [64, 8192], P(None, 'mod'), may hold values from -0.0625 to 0.0625
- proj_out: bfloat16 [64, 28672], P(None, 'mod'), may hold values from -0.03125 to 0.03125
- doc_lengths: int32 [4, 16], P('seq'), may hold values from 1 to 640, as said below
Outputs:
- sketches: bfloat16 [4, 16, 4096], P('seq', ('ctx', 'mod'))
- fisher: float32 [4096, 4096], P('ctx', ('mod', 'seq'))
The draws below stay inside these ranges and needn't reach their ends.
Inputs may be any that keep to these rules, and one draw needn't show every extreme that they name: `doc_lengths`: row s holds the lengths of the 16 documents packed one after another into sequence s; each row sums to 1024; the first document of every sequence is the longest and has exactly the largest length.
All inputs are finite; a program needn't handle non-finite values.
Results may differ from the reference program's by a relative error of at most 0.0076.
Values may be sent and summed in bfloat16 or wider, within the bound.
No kernel may reach another device: no remote copies, remote signals or barrier semaphores. Data moves between devices by JAX's collectives and lax.ppermute only.
A program may use at most 64 MiB of HBM per device.

```python
import jax
import jax.numpy as jnp
from jax import lax

D = 8192
FF = 28672
RANK = 64
TOK_DEV = 256
SEQS = 4
LEN = 1024
DOCS = 16
N_MOD = 2


def draw_doc_lengths(key, part):
    longest = LEN // 2 + TOK_DEV // N_MOD
    spare = LEN - longest - (DOCS - 1)
    cuts = jax.random.randint(key, (SEQS, DOCS - 2), 0, spare + 1).astype(jnp.int32)
    cuts = jnp.sort(cuts, axis=1)
    edges = jnp.concatenate([jnp.zeros((SEQS, 1), jnp.int32), cuts, jnp.full((SEQS, 1), spare, jnp.int32)], axis=1)
    others = (1 + edges[:, 1:] - edges[:, :-1]).astype(jnp.int32)
    first = jnp.full((SEQS, 1), longest, jnp.int32)
    return jnp.concatenate([first, others], axis=1).astype(jnp.int32)


def block_scale(key, shape, shards, least, high):
    level, own = 1.0, jax.random.fold_in(key, 6)
    for dim, blocks in shards:
        draws = jnp.exp(jax.random.uniform(jax.random.fold_in(own, dim), (blocks,), jnp.float32, least / len(shards), high / len(shards)))
        level = level * jnp.repeat(draws, shape[dim] // blocks).reshape([-1 if axis == dim else 1 for axis in range(len(shape))])
    return level


def normal_values(key, dims, scale, reach, pieces=(), kind=jnp.bfloat16):
    array = jax.random.normal(key, dims, jnp.float32) * scale
    if len(pieces) > 0:
        array = block_scale(key, dims, pieces, -0.22, 0.18) * array
    return jnp.clip(array, min=-reach, max=reach).astype(kind)


def setup_inputs(seed: int = 0) -> dict:
    key_of = jax.random.split(jax.random.key(seed), 6)
    return {
        "inputs": normal_values(key_of[0], (SEQS, LEN, D), 1.0, 6.0, ((0, 4), (1, 4), (2, 2))),
        "out_grads": normal_values(key_of[1], (SEQS, LEN, FF), 1.0, 6.0, ((0, 4), (1, 4), (2, 2))),
        "proj_in": normal_values(key_of[2], (RANK, D), D ** -0.5, 0.0625, ((1, 2),)),
        "proj_out": normal_values(key_of[3], (RANK, FF), FF ** -0.5, 0.03125, ((1, 2),)),
        "doc_lengths": draw_doc_lengths(jax.random.fold_in(key_of[5], 71), 0),
    }


def sketch_sequence(token_rows, grad_rows, lengths, proj_in, proj_out):
    in_proj = jnp.dot(token_rows, proj_in.T, preferred_element_type=jnp.float32).astype(jnp.bfloat16)
    out_proj = jnp.dot(grad_rows, proj_out.T, preferred_element_type=jnp.float32).astype(jnp.bfloat16)
    doc_ends = jnp.cumsum(lengths).astype(jnp.int32)
    position = jnp.arange(LEN, dtype=jnp.int32)
    doc_index = lax.optimization_barrier(jnp.sum((position[:, None] >= doc_ends[None, :]).astype(jnp.int32), axis=1)).astype(jnp.int32)
    products = (out_proj.astype(jnp.float32)[:, :, None] * in_proj.astype(jnp.float32)[:, None, :]).reshape(LEN, RANK * RANK)
    doc_sum = jax.ops.segment_sum(products, doc_index, num_segments=DOCS)
    scaled = doc_sum / jnp.sqrt(lengths.astype(jnp.float32))[:, None]
    return scaled.astype(jnp.bfloat16)

def reference(inputs, out_grads, proj_in, proj_out, doc_lengths):

    def one_sequence(operands):
        return sketch_sequence(operands[0], operands[1], operands[2], proj_in, proj_out)
    sketches = lax.map(one_sequence, (inputs, out_grads, doc_lengths))
    stacked = sketches.reshape(SEQS * DOCS, RANK * RANK)
    fisher = jnp.dot(stacked.T, stacked, preferred_element_type=jnp.float32) / (SEQS * DOCS)
    return (sketches, fisher)
```

```python
import jax
import jax.numpy as jnp
from jax import lax
from jax.experimental import pallas as pl
from jax.experimental.pallas import tpu as pltpu
from jax.sharding import PartitionSpec as P


LANES = 128
F32 = jnp.float32
BF16 = jnp.bfloat16
BOTH_LAST = (((1,), (1,)), ((), ()))
BOTH_FIRST = (((0,), (0,)), ((), ()))
IN_VMEM = pl.BlockSpec(memory_space=pltpu.VMEM)
IN_HBM = pl.BlockSpec(memory_space=pltpu.HBM)


def vmem(array):
    return pltpu.with_memory_space_constraint(array, pltpu.VMEM)


def chunk_of(width):
    return max(size for size in (2048, 1024, 512, 256, 128) if width % size == 0)


def project_kernel(x_hbm, g_hbm, pi_hbm, po_hbm, out_ref, x, g, pi, po, sems):
    copies = []

    def fetch(source, target):
        copy = pltpu.make_async_copy(source, target, sems.at[len(copies)])
        copy.start()
        copies.append(copy)
        return copy

    plans = []
    for data_hbm, weight_hbm, data, weight in ((x_hbm, pi_hbm, x, pi), (g_hbm, po_hbm, g, po)):
        size = data.shape[2]
        waits = []
        for step in range(data.shape[0]):
            columns = pl.ds(step * size, size)
            waits.append(
                (
                    fetch(weight_hbm.at[:, columns], weight.at[step]),
                    fetch(data_hbm.at[0, :, columns], data.at[step]),
                )
            )
        plans.append((waits, data, weight))
    parts = []
    for waits, data, weight in plans:
        total = None
        for step, pair in enumerate(waits):
            for copy in pair:
                copy.wait()
            product = lax.dot_general(
                weight[step], data[step], BOTH_LAST, preferred_element_type=F32
            )
            total = product if total is None else total + product
        parts.append(total)
    in_part, out_part = parts
    out_ref[...] = jnp.concatenate([out_part, in_part], axis=0).astype(BF16)


def project(inputs, out_grads, proj_in, proj_out):
    ranks, tokens = proj_in.shape[0], inputs.shape[1]
    scratch = []
    steps = 0
    for width, rows in (
        (inputs.shape[2], tokens),
        (out_grads.shape[2], tokens),
        (proj_in.shape[1], ranks),
        (proj_out.shape[1], ranks),
    ):
        size = chunk_of(width)
        scratch.append(pltpu.VMEM((width // size, rows, size), BF16))
        steps += width // size
    return pl.pallas_call(
        project_kernel,
        out_shape=pltpu.VMEM((2 * ranks, tokens), BF16),
        in_specs=[IN_HBM] * 4,
        out_specs=IN_VMEM,
        scratch_shapes=scratch + [pltpu.SemaphoreType.DMA((steps,))],
        name="project",
    )(inputs, out_grads, proj_in, proj_out)


def sketch_kernel(n_ctx, n_mod, n_seq, *refs):
    parts = refs[: 2 * n_ctx]
    lengths_ref = refs[2 * n_ctx]
    own_ref = refs[2 * n_ctx + 1]
    share_refs = refs[2 * n_ctx + 2 : 2 * n_ctx + 2 + n_seq]
    rows_t, weighted, total, sketch = refs[2 * n_ctx + 2 + n_seq :]
    ctx, mod, seq = lax.axis_index("ctx"), lax.axis_index("mod"), lax.axis_index("seq")
    docs = lengths_ref.shape[1]
    ranks, tokens = rows_t.shape[1] // 2, rows_t.shape[2]
    pairs = sketch.shape[0]

    for chunk in range(n_ctx):
        rows_t[chunk] = parts[2 * chunk][...].astype(F32) + parts[2 * chunk + 1][...].astype(F32)

    lengths = jnp.broadcast_to(lengths_ref[...].astype(F32), (docs, docs))
    doc = lax.broadcasted_iota(jnp.int32, (docs, docs), 0)
    other = lax.broadcasted_iota(jnp.int32, (docs, docs), 1)
    ends = jnp.sum(jnp.where(other <= doc, lengths, 0.0), axis=1, keepdims=True)
    own_lengths = jnp.sum(jnp.where(other == doc, lengths, 0.0), axis=1, keepdims=True)
    starts = ends - own_lengths
    local = lax.broadcasted_iota(jnp.int32, (docs, tokens), 1)

    def add_chunk(chunk, slot):
        position = (local + jnp.bitwise_xor(ctx, chunk) * tokens).astype(F32)
        inside = ((position >= starts) & (position < ends)).astype(F32)
        for pair in range(pairs):
            for half in range(2):
                row = rows_t[chunk, pl.ds(2 * pair + half, 1), :].astype(BF16).astype(F32)
                weighted[slot, pl.ds(pair * docs, docs), pl.ds(half * tokens, tokens)] = (
                    inside * row
                ).astype(BF16)
        in_rows = rows_t[chunk, pl.ds(ranks, ranks), :].astype(BF16)
        none = jnp.zeros_like(in_rows)
        spread = jnp.concatenate(
            [jnp.concatenate([in_rows, none], axis=1), jnp.concatenate([none, in_rows], axis=1)],
            axis=0,
        )
        return lax.dot_general(weighted[slot], spread, BOTH_LAST, preferred_element_type=F32)

    if n_ctx <= 4:
        summed = add_chunk(0, 0)
        for chunk in range(1, n_ctx):
            summed += add_chunk(chunk, chunk % 2)
        total[...] = summed
    else:
        total[...] = jnp.zeros_like(total)

        def step(chunk, carry):
            total[...] += add_chunk(chunk, 0)
            return carry

        lax.fori_loop(0, n_ctx, step, 0)

    root = jnp.sqrt(own_lengths)
    share = own_ref.shape[1]
    group = ctx * n_mod + mod
    for pair in range(pairs):
        rows = pl.ds(pair * docs, docs)
        scaled = total[rows, :] / root
        total[rows, :] = scaled
        sketch[pair] = scaled.astype(BF16)
    for pair in range(pairs):
        own = total[pl.ds(pair * docs + group * share, share), :]
        own_ref[0, :, pl.ds(pair * LANES, LANES)] = own.astype(BF16)
    row_pairs = pairs // n_ctx
    column_pairs = pairs // (n_mod * n_seq)
    for step, share_ref in enumerate(share_refs):
        first = (mod * n_seq + jnp.bitwise_xor(seq, step)) * column_pairs
        for at in range(row_pairs):
            share_ref[at] = sketch[ctx * row_pairs + at]
        for at in range(column_pairs):
            share_ref[row_pairs + at] = sketch[first + at]


def sketches_of(parts, doc_lengths, n_ctx, n_mod, n_seq):
    docs = doc_lengths.shape[1]
    ranks, tokens = parts[0].shape[0] // 2, parts[0].shape[1]
    features = ranks * ranks
    pairs = features // LANES
    blocks = pairs // n_ctx + pairs // (n_mod * n_seq)
    share = docs // (n_ctx * n_mod)

    def body(*refs):
        sketch_kernel(n_ctx, n_mod, n_seq, *refs)

    return pl.pallas_call(
        body,
        out_shape=[pltpu.VMEM((1, share, features), BF16)]
        + [pltpu.VMEM((blocks, docs, LANES), BF16)] * n_seq,
        in_specs=[IN_VMEM] * (len(parts) + 1),
        out_specs=[IN_VMEM] * (1 + n_seq),
        scratch_shapes=[
            pltpu.VMEM((n_ctx, 2 * ranks, tokens), F32),
            pltpu.VMEM((2, pairs * docs, 2 * tokens), BF16),
            pltpu.VMEM((pairs * docs, LANES), F32),
            pltpu.VMEM((pairs, docs, LANES), BF16),
        ],
        name="sketch",
    )(*[vmem(part) if n_ctx <= 4 else part for part in parts], vmem(doc_lengths))


def fisher_kernel(row_pairs, total_docs, *refs):
    shares, out_hbm, tiles, sems = refs[:-3], refs[-3], refs[-2], refs[-1]
    blocks = shares[0].shape[0]

    def over_docs(at):
        return jnp.concatenate([share[at] for share in shares], axis=0)

    columns = jnp.concatenate([over_docs(at) for at in range(row_pairs, blocks)], axis=1)
    copies = []
    for at in range(row_pairs):
        tile = lax.dot_general(over_docs(at), columns, BOTH_FIRST, preferred_element_type=F32)
        tiles[at] = tile / total_docs
        copy = pltpu.make_async_copy(
            tiles.at[at], out_hbm.at[pl.ds(at * LANES, LANES), :], sems.at[at]
        )
        copy.start()
        copies.append(copy)
    for copy in copies:
        copy.wait()


def fisher_of(shares, row_pairs, total_docs):
    width = (shares[0].shape[0] - row_pairs) * LANES

    def body(*refs):
        fisher_kernel(row_pairs, total_docs, *refs)

    return pl.pallas_call(
        body,
        out_shape=pltpu.HBM((row_pairs * LANES, width), F32),
        in_specs=[IN_VMEM] * len(shares),
        out_specs=IN_HBM,
        scratch_shapes=[
            pltpu.VMEM((row_pairs, LANES, width), F32),
            pltpu.SemaphoreType.DMA((row_pairs,)),
        ],
        name="fisher",
    )(*[vmem(share) for share in shares])


def per_device(inputs, out_grads, proj_in, proj_out, doc_lengths):
    n_ctx, n_mod, n_seq = (lax.axis_size(name) for name in ("ctx", "mod", "seq"))

    def from_plane(array, ctx_step, mod_step):
        pairs = [
            (ctx * n_mod + mod, (ctx ^ ctx_step) * n_mod + (mod ^ mod_step))
            for ctx in range(n_ctx)
            for mod in range(n_mod)
        ]
        return lax.ppermute(array, ("ctx", "mod"), pairs)

    def from_seq(array, step):
        return lax.ppermute(array, "seq", [(seq, seq ^ step) for seq in range(n_seq)])

    own = project(inputs, out_grads, proj_in, proj_out)
    parts = [None] * (2 * n_ctx)
    for step in range(0, n_ctx, 2):
        for mod_step in range(2):
            near = own if step + mod_step == 0 else from_plane(own, step, mod_step)
            parts[2 * step + mod_step] = near
            parts[2 * step + 2 + mod_step] = from_plane(near, 1, 0)
    made = sketches_of(parts, doc_lengths, n_ctx, n_mod, n_seq)
    sketch, shares = made[0], made[1:]
    gathered = [shares[0]] + [from_seq(shares[step], step) for step in range(1, n_seq)]
    ranks = proj_in.shape[0]
    row_pairs = ranks * ranks // LANES // n_ctx
    fisher = fisher_of(gathered, row_pairs, doc_lengths.shape[1] * n_seq)
    return (sketch, fisher)


def solution(mesh):
    placed = (
        P("seq", "ctx", "mod"),
        P("seq", "ctx", "mod"),
        P(None, "mod"),
        P(None, "mod"),
        P("seq", None),
    )
    return jax.shard_map(
        per_device,
        mesh=mesh,
        in_specs=placed,
        out_specs=(P("seq", ("ctx", "mod"), None), P("ctx", ("mod", "seq"))),
        check_vma=False,
    )
```

```python
import jax
import jax.numpy as jnp
from jax import lax
from jax.experimental import pallas as pl
from jax.experimental.pallas import tpu as pltpu
from jax.sharding import PartitionSpec as P


LANES = 128
F32 = jnp.float32
BF16 = jnp.bfloat16
BOTH_LAST = (((1,), (1,)), ((), ()))
BOTH_FIRST = (((0,), (0,)), ((), ()))
IN_VMEM = pl.BlockSpec(memory_space=pltpu.VMEM)
IN_HBM = pl.BlockSpec(memory_space=pltpu.HBM)


def vmem(array):
    return pltpu.with_memory_space_constraint(array, pltpu.VMEM)


def chunk_of(width):
    return max(size for size in (2048, 1024, 512, 256, 128) if width % size == 0)


def project_kernel(x_hbm, g_hbm, pi_hbm, po_hbm, out_ref, x, g, pi, po, sems):
    copies = []

    def fetch(source, target):
        copy = pltpu.make_async_copy(source, target, sems.at[len(copies)])
        copy.start()
        copies.append(copy)
        return copy

    plans = []
    for data_hbm, weight_hbm, data, weight in ((x_hbm, pi_hbm, x, pi), (g_hbm, po_hbm, g, po)):
        size = data.shape[2]
        waits = []
        for step in range(data.shape[0]):
            columns = pl.ds(step * size, size)
            waits.append(
                (
                    fetch(weight_hbm.at[:, columns], weight.at[step]),
                    fetch(data_hbm.at[0, :, columns], data.at[step]),
                )
            )
        plans.append((waits, data, weight))
    parts = []
    for waits, data, weight in plans:
        half = data.shape[2] // 2
        by_rank, by_position = [], []
        for step, pair in enumerate(waits):
            for copy in pair:
                copy.wait()
            by_rank.append(
                lax.dot_general(
                    weight[step, :, :half], data[step, :, :half], BOTH_LAST, preferred_element_type=F32
                )
            )
            by_position.append(
                lax.dot_general(
                    data[step, :, half:], weight[step, :, half:], BOTH_LAST, preferred_element_type=F32
                )
            )
        parts.append((sum(by_rank[1:], by_rank[0]), sum(by_position[1:], by_position[0])))
    (in_rank, in_position), (out_rank, out_position) = parts
    by_rank = jnp.concatenate([out_rank, in_rank], axis=0)
    by_position = jnp.concatenate([out_position, in_position], axis=1)
    out_ref[...] = (by_rank + by_position.T).astype(BF16)


def project(inputs, out_grads, proj_in, proj_out):
    ranks, tokens = proj_in.shape[0], inputs.shape[1]
    scratch = []
    steps = 0
    for width, rows in (
        (inputs.shape[2], tokens),
        (out_grads.shape[2], tokens),
        (proj_in.shape[1], ranks),
        (proj_out.shape[1], ranks),
    ):
        size = chunk_of(width)
        scratch.append(pltpu.VMEM((width // size, rows, size), BF16))
        steps += width // size
    return pl.pallas_call(
        project_kernel,
        out_shape=pltpu.VMEM((2 * ranks, tokens), BF16),
        in_specs=[IN_HBM] * 4,
        out_specs=IN_VMEM,
        scratch_shapes=scratch + [pltpu.SemaphoreType.DMA((steps,))],
        name="project",
    )(inputs, out_grads, proj_in, proj_out)


def sketch_kernel(n_ctx, n_mod, n_seq, *refs):
    parts = refs[: 2 * n_ctx]
    lengths_ref = refs[2 * n_ctx]
    own_ref = refs[2 * n_ctx + 1]
    share_refs = refs[2 * n_ctx + 2 : 2 * n_ctx + 2 + n_seq]
    rows_t, weighted, total, sketch = refs[2 * n_ctx + 2 + n_seq :]
    ctx, mod, seq = lax.axis_index("ctx"), lax.axis_index("mod"), lax.axis_index("seq")
    docs = lengths_ref.shape[1]
    ranks, tokens = rows_t.shape[1] // 2, rows_t.shape[2]
    pairs = sketch.shape[0]

    for chunk in range(n_ctx):
        rows_t[chunk] = parts[2 * chunk][...].astype(F32) + parts[2 * chunk + 1][...].astype(F32)

    lengths = jnp.broadcast_to(lengths_ref[...].astype(F32), (docs, docs))
    doc = lax.broadcasted_iota(jnp.int32, (docs, docs), 0)
    other = lax.broadcasted_iota(jnp.int32, (docs, docs), 1)
    ends = jnp.sum(jnp.where(other <= doc, lengths, 0.0), axis=1, keepdims=True)
    own_lengths = jnp.sum(jnp.where(other == doc, lengths, 0.0), axis=1, keepdims=True)
    starts = ends - own_lengths
    local = lax.broadcasted_iota(jnp.int32, (docs, tokens), 1)

    def add_chunk(chunk, slot):
        position = (local + jnp.bitwise_xor(ctx, chunk) * tokens).astype(F32)
        inside = ((position >= starts) & (position < ends)).astype(F32)
        for pair in range(pairs):
            for half in range(2):
                row = rows_t[chunk, pl.ds(2 * pair + half, 1), :].astype(BF16).astype(F32)
                weighted[slot, pl.ds(pair * docs, docs), pl.ds(half * tokens, tokens)] = (
                    inside * row
                ).astype(BF16)
        in_rows = rows_t[chunk, pl.ds(ranks, ranks), :].astype(BF16)
        none = jnp.zeros_like(in_rows)
        spread = jnp.concatenate(
            [jnp.concatenate([in_rows, none], axis=1), jnp.concatenate([none, in_rows], axis=1)],
            axis=0,
        )
        return lax.dot_general(weighted[slot], spread, BOTH_LAST, preferred_element_type=F32)

    if n_ctx <= 4:
        summed = add_chunk(0, 0)
        for chunk in range(1, n_ctx):
            summed += add_chunk(chunk, chunk % 2)
        total[...] = summed
    else:
        total[...] = jnp.zeros_like(total)

        def step(chunk, carry):
            total[...] += add_chunk(chunk, 0)
            return carry

        lax.fori_loop(0, n_ctx, step, 0)

    root = jnp.sqrt(own_lengths)
    share = own_ref.shape[1]
    group = ctx * n_mod + mod
    for pair in range(pairs):
        rows = pl.ds(pair * docs, docs)
        scaled = total[rows, :] / root
        total[rows, :] = scaled
        sketch[pair] = scaled.astype(BF16)
    for pair in range(pairs):
        own = total[pl.ds(pair * docs + group * share, share), :]
        own_ref[0, :, pl.ds(pair * LANES, LANES)] = own.astype(BF16)
    row_pairs = pairs // n_ctx
    column_pairs = pairs // (n_mod * n_seq)
    for step, share_ref in enumerate(share_refs):
        first = (mod * n_seq + jnp.bitwise_xor(seq, step)) * column_pairs
        for at in range(row_pairs):
            share_ref[at] = sketch[ctx * row_pairs + at]
        for at in range(column_pairs):
            share_ref[row_pairs + at] = sketch[first + at]


def sketches_of(parts, doc_lengths, n_ctx, n_mod, n_seq):
    docs = doc_lengths.shape[1]
    ranks, tokens = parts[0].shape[0] // 2, parts[0].shape[1]
    features = ranks * ranks
    pairs = features // LANES
    blocks = pairs // n_ctx + pairs // (n_mod * n_seq)
    share = docs // (n_ctx * n_mod)

    def body(*refs):
        sketch_kernel(n_ctx, n_mod, n_seq, *refs)

    return pl.pallas_call(
        body,
        out_shape=[pltpu.VMEM((1, share, features), BF16)]
        + [pltpu.VMEM((blocks, docs, LANES), BF16)] * n_seq,
        in_specs=[IN_VMEM] * (len(parts) + 1),
        out_specs=[IN_VMEM] * (1 + n_seq),
        scratch_shapes=[
            pltpu.VMEM((n_ctx, 2 * ranks, tokens), F32),
            pltpu.VMEM((2, pairs * docs, 2 * tokens), BF16),
            pltpu.VMEM((pairs * docs, LANES), F32),
            pltpu.VMEM((pairs, docs, LANES), BF16),
        ],
        name="sketch",
    )(*[vmem(part) if n_ctx <= 4 else part for part in parts], vmem(doc_lengths))


def fisher_kernel(row_pairs, total_docs, *refs):
    shares, out_hbm, tiles, sems = refs[:-3], refs[-3], refs[-2], refs[-1]
    blocks = shares[0].shape[0]

    def over_docs(at):
        return jnp.concatenate([share[at] for share in shares], axis=0)

    columns = jnp.concatenate([over_docs(at) for at in range(row_pairs, blocks)], axis=1)
    copies = []
    for at in range(row_pairs):
        tile = lax.dot_general(over_docs(at), columns, BOTH_FIRST, preferred_element_type=F32)
        tiles[at] = tile / total_docs
        copy = pltpu.make_async_copy(
            tiles.at[at], out_hbm.at[pl.ds(at * LANES, LANES), :], sems.at[at]
        )
        copy.start()
        copies.append(copy)
    for copy in copies:
        copy.wait()


def fisher_of(shares, row_pairs, total_docs):
    width = (shares[0].shape[0] - row_pairs) * LANES

    def body(*refs):
        fisher_kernel(row_pairs, total_docs, *refs)

    return pl.pallas_call(
        body,
        out_shape=pltpu.HBM((row_pairs * LANES, width), F32),
        in_specs=[IN_VMEM] * len(shares),
        out_specs=IN_HBM,
        scratch_shapes=[
            pltpu.VMEM((row_pairs, LANES, width), F32),
            pltpu.SemaphoreType.DMA((row_pairs,)),
        ],
        name="fisher",
    )(*[vmem(share) for share in shares])


def per_device(inputs, out_grads, proj_in, proj_out, doc_lengths):
    n_ctx, n_mod, n_seq = (lax.axis_size(name) for name in ("ctx", "mod", "seq"))

    def from_plane(array, ctx_step, mod_step):
        pairs = [
            (ctx * n_mod + mod, (ctx ^ ctx_step) * n_mod + (mod ^ mod_step))
            for ctx in range(n_ctx)
            for mod in range(n_mod)
        ]
        return lax.ppermute(array, ("ctx", "mod"), pairs)

    def from_seq(array, step):
        return lax.ppermute(array, "seq", [(seq, seq ^ step) for seq in range(n_seq)])

    own = project(inputs, out_grads, proj_in, proj_out)
    parts = [None] * (2 * n_ctx)
    for step in range(0, n_ctx, 2):
        for mod_step in range(2):
            near = own if step + mod_step == 0 else from_plane(own, step, mod_step)
            parts[2 * step + mod_step] = near
            parts[2 * step + 2 + mod_step] = from_plane(near, 1, 0)
    made = sketches_of(parts, doc_lengths, n_ctx, n_mod, n_seq)
    sketch, shares = made[0], made[1:]
    gathered = [shares[0]] + [from_seq(shares[step], step) for step in range(1, n_seq)]
    ranks = proj_in.shape[0]
    row_pairs = ranks * ranks // LANES // n_ctx
    fisher = fisher_of(gathered, row_pairs, doc_lengths.shape[1] * n_seq)
    return (sketch, fisher)


def solution(mesh):
    placed = (
        P("seq", "ctx", "mod"),
        P("seq", "ctx", "mod"),
        P(None, "mod"),
        P(None, "mod"),
        P("seq", None),
    )
    return jax.shard_map(
        per_device,
        mesh=mesh,
        in_specs=placed,
        out_specs=(P("seq", ("ctx", "mod"), None), P("ctx", ("mod", "seq"))),
        check_vma=False,
    )
```

```python
import jax
import jax.numpy as jnp
from jax import lax
from jax.experimental import pallas as pl
from jax.experimental.pallas import tpu as pltpu
from jax.sharding import PartitionSpec as P


LANES = 128
CODE_BITS = 13.0
POWER_ROWS = 16
F32 = jnp.float32
BF16 = jnp.bfloat16
BOTH_LAST = (((1,), (1,)), ((), ()))
BOTH_FIRST = (((0,), (0,)), ((), ()))
IN_VMEM = pl.BlockSpec(memory_space=pltpu.VMEM)
IN_HBM = pl.BlockSpec(memory_space=pltpu.HBM)


def vmem(array):
    return pltpu.with_memory_space_constraint(array, pltpu.VMEM)


def chunk_of(width):
    return max(size for size in (2048, 1024, 512, 256, 128) if width % size == 0)


def project_kernel(x_hbm, g_hbm, pi_hbm, po_hbm, out_ref, x, g, pi, po, sems):
    copies = []

    def fetch(source, target):
        copy = pltpu.make_async_copy(source, target, sems.at[len(copies)])
        copy.start()
        copies.append(copy)
        return copy

    plans = []
    for data_hbm, weight_hbm, data, weight in ((x_hbm, pi_hbm, x, pi), (g_hbm, po_hbm, g, po)):
        size = data.shape[2]
        waits = []
        for step in range(data.shape[0]):
            columns = pl.ds(step * size, size)
            waits.append(
                (
                    fetch(weight_hbm.at[:, columns], weight.at[step]),
                    fetch(data_hbm.at[0, :, columns], data.at[step]),
                )
            )
        plans.append((waits, data, weight))
    parts = []
    for waits, data, weight in plans:
        half = data.shape[2] // 2
        by_rank, by_position = [], []
        for step, pair in enumerate(waits):
            for copy in pair:
                copy.wait()
            by_rank.append(
                lax.dot_general(
                    weight[step, :, :half], data[step, :, :half], BOTH_LAST, preferred_element_type=F32
                )
            )
            by_position.append(
                lax.dot_general(
                    data[step, :, half:], weight[step, :, half:], BOTH_LAST, preferred_element_type=F32
                )
            )
        parts.append((sum(by_rank[1:], by_rank[0]), sum(by_position[1:], by_position[0])))
    (in_rank, in_position), (out_rank, out_position) = parts
    by_rank = jnp.concatenate([out_rank, in_rank], axis=0)
    by_position = jnp.concatenate([out_position, in_position], axis=1)
    summed = by_rank + by_position.T
    ranks = summed.shape[0] // 2
    for side in range(2):
        rows = summed[side * ranks : (side + 1) * ranks]
        peak = jnp.maximum(jnp.max(jnp.abs(rows), axis=0, keepdims=True), 1e-30)
        power = jnp.floor(jnp.log2(peak))
        coded = jnp.round(rows * jnp.exp2(CODE_BITS - power))
        out_ref[pl.ds(side * ranks, ranks), :] = coded.astype(jnp.int32).astype(jnp.int16)
        powers = power if side == 0 else jnp.where(top, powers, power)
        top = lax.broadcasted_iota(jnp.int32, (POWER_ROWS, rows.shape[1]), 0) < POWER_ROWS // 2
    out_ref[pl.ds(2 * ranks, POWER_ROWS), :] = powers.astype(jnp.int32).astype(jnp.int16)


def decoded(part_ref):
    ranks = (part_ref.shape[0] - POWER_ROWS) // 2
    powers = part_ref[pl.ds(2 * ranks, POWER_ROWS), :].astype(jnp.int32).astype(F32)
    steps = jnp.exp2(powers - CODE_BITS)
    halves = []
    for side in range(2):
        codes = part_ref[pl.ds(side * ranks, ranks), :].astype(jnp.int32).astype(F32)
        at = side * (POWER_ROWS // 2)
        halves.append(codes * steps[at : at + 1])
    return jnp.concatenate(halves, axis=0)


def project(inputs, out_grads, proj_in, proj_out):
    ranks, tokens = proj_in.shape[0], inputs.shape[1]
    scratch = []
    steps = 0
    for width, rows in (
        (inputs.shape[2], tokens),
        (out_grads.shape[2], tokens),
        (proj_in.shape[1], ranks),
        (proj_out.shape[1], ranks),
    ):
        size = chunk_of(width)
        scratch.append(pltpu.VMEM((width // size, rows, size), BF16))
        steps += width // size
    return pl.pallas_call(
        project_kernel,
        out_shape=pltpu.VMEM((2 * ranks + POWER_ROWS, tokens), jnp.int16),
        in_specs=[IN_HBM] * 4,
        out_specs=IN_VMEM,
        scratch_shapes=scratch + [pltpu.SemaphoreType.DMA((steps,))],
        name="project",
    )(inputs, out_grads, proj_in, proj_out)


def sketch_kernel(n_ctx, n_mod, n_seq, *refs):
    parts = refs[: 2 * n_ctx]
    lengths_ref = refs[2 * n_ctx]
    own_ref = refs[2 * n_ctx + 1]
    share_refs = refs[2 * n_ctx + 2 : 2 * n_ctx + 2 + n_seq]
    rows_t, weighted, total, sketch = refs[2 * n_ctx + 2 + n_seq :]
    ctx, mod, seq = lax.axis_index("ctx"), lax.axis_index("mod"), lax.axis_index("seq")
    docs = lengths_ref.shape[1]
    ranks, tokens = rows_t.shape[1] // 2, rows_t.shape[2]
    pairs = sketch.shape[0]

    for chunk in range(n_ctx):
        rows_t[chunk] = decoded(parts[2 * chunk]) + decoded(parts[2 * chunk + 1])

    lengths = jnp.broadcast_to(lengths_ref[...].astype(F32), (docs, docs))
    doc = lax.broadcasted_iota(jnp.int32, (docs, docs), 0)
    other = lax.broadcasted_iota(jnp.int32, (docs, docs), 1)
    ends = jnp.sum(jnp.where(other <= doc, lengths, 0.0), axis=1, keepdims=True)
    own_lengths = jnp.sum(jnp.where(other == doc, lengths, 0.0), axis=1, keepdims=True)
    starts = ends - own_lengths
    local = lax.broadcasted_iota(jnp.int32, (docs, tokens), 1)

    def add_chunk(chunk, slot):
        position = (local + jnp.bitwise_xor(ctx, chunk) * tokens).astype(F32)
        inside = ((position >= starts) & (position < ends)).astype(F32)
        for pair in range(pairs):
            for half in range(2):
                row = rows_t[chunk, pl.ds(2 * pair + half, 1), :].astype(BF16).astype(F32)
                weighted[slot, pl.ds(pair * docs, docs), pl.ds(half * tokens, tokens)] = (
                    inside * row
                ).astype(BF16)
        in_rows = rows_t[chunk, pl.ds(ranks, ranks), :].astype(BF16)
        none = jnp.zeros_like(in_rows)
        spread = jnp.concatenate(
            [jnp.concatenate([in_rows, none], axis=1), jnp.concatenate([none, in_rows], axis=1)],
            axis=0,
        )
        return lax.dot_general(weighted[slot], spread, BOTH_LAST, preferred_element_type=F32)

    if n_ctx <= 4:
        summed = add_chunk(0, 0)
        for chunk in range(1, n_ctx):
            summed += add_chunk(chunk, chunk % 2)
        total[...] = summed
    else:
        total[...] = jnp.zeros_like(total)

        def step(chunk, carry):
            total[...] += add_chunk(chunk, 0)
            return carry

        lax.fori_loop(0, n_ctx, step, 0)

    root = jnp.sqrt(own_lengths)
    share = own_ref.shape[1]
    group = ctx * n_mod + mod
    for pair in range(pairs):
        rows = pl.ds(pair * docs, docs)
        scaled = total[rows, :] / root
        total[rows, :] = scaled
        sketch[pair] = scaled.astype(BF16)
    for pair in range(pairs):
        own = total[pl.ds(pair * docs + group * share, share), :]
        own_ref[0, :, pl.ds(pair * LANES, LANES)] = own.astype(BF16)
    row_pairs = pairs // n_ctx
    column_pairs = pairs // (n_mod * n_seq)
    for step, share_ref in enumerate(share_refs):
        first = (mod * n_seq + jnp.bitwise_xor(seq, step)) * column_pairs
        for at in range(row_pairs):
            share_ref[at] = sketch[ctx * row_pairs + at]
        for at in range(column_pairs):
            share_ref[row_pairs + at] = sketch[first + at]


def sketches_of(parts, doc_lengths, n_ctx, n_mod, n_seq):
    docs = doc_lengths.shape[1]
    ranks, tokens = (parts[0].shape[0] - POWER_ROWS) // 2, parts[0].shape[1]
    features = ranks * ranks
    pairs = features // LANES
    blocks = pairs // n_ctx + pairs // (n_mod * n_seq)
    share = docs // (n_ctx * n_mod)

    def body(*refs):
        sketch_kernel(n_ctx, n_mod, n_seq, *refs)

    return pl.pallas_call(
        body,
        out_shape=[pltpu.VMEM((1, share, features), BF16)]
        + [pltpu.VMEM((blocks, docs, LANES), BF16)] * n_seq,
        in_specs=[IN_VMEM] * (len(parts) + 1),
        out_specs=[IN_VMEM] * (1 + n_seq),
        scratch_shapes=[
            pltpu.VMEM((n_ctx, 2 * ranks, tokens), F32),
            pltpu.VMEM((2, pairs * docs, 2 * tokens), BF16),
            pltpu.VMEM((pairs * docs, LANES), F32),
            pltpu.VMEM((pairs, docs, LANES), BF16),
        ],
        name="sketch",
    )(*[vmem(part) if n_ctx <= 4 else part for part in parts], vmem(doc_lengths))


def fisher_kernel(row_pairs, total_docs, *refs):
    shares, out_hbm, tiles, sems = refs[:-3], refs[-3], refs[-2], refs[-1]
    blocks = shares[0].shape[0]

    def over_docs(at):
        return jnp.concatenate([share[at] for share in shares], axis=0)

    columns = jnp.concatenate([over_docs(at) for at in range(row_pairs, blocks)], axis=1)
    copies = []
    for at in range(row_pairs):
        tile = lax.dot_general(over_docs(at), columns, BOTH_FIRST, preferred_element_type=F32)
        tiles[at] = tile / total_docs
        copy = pltpu.make_async_copy(
            tiles.at[at], out_hbm.at[pl.ds(at * LANES, LANES), :], sems.at[at]
        )
        copy.start()
        copies.append(copy)
    for copy in copies:
        copy.wait()


def fisher_of(shares, row_pairs, total_docs):
    width = (shares[0].shape[0] - row_pairs) * LANES

    def body(*refs):
        fisher_kernel(row_pairs, total_docs, *refs)

    return pl.pallas_call(
        body,
        out_shape=pltpu.HBM((row_pairs * LANES, width), F32),
        in_specs=[IN_VMEM] * len(shares),
        out_specs=IN_HBM,
        scratch_shapes=[
            pltpu.VMEM((row_pairs, LANES, width), F32),
            pltpu.SemaphoreType.DMA((row_pairs,)),
        ],
        name="fisher",
    )(*[vmem(share) for share in shares])


def per_device(inputs, out_grads, proj_in, proj_out, doc_lengths):
    n_ctx, n_mod, n_seq = (lax.axis_size(name) for name in ("ctx", "mod", "seq"))

    def from_plane(array, ctx_step, mod_step):
        pairs = [
            (ctx * n_mod + mod, (ctx ^ ctx_step) * n_mod + (mod ^ mod_step))
            for ctx in range(n_ctx)
            for mod in range(n_mod)
        ]
        return lax.ppermute(array, ("ctx", "mod"), pairs)

    def from_seq(array, step):
        return lax.ppermute(array, "seq", [(seq, seq ^ step) for seq in range(n_seq)])

    own = project(inputs, out_grads, proj_in, proj_out)
    parts = [None] * (2 * n_ctx)
    for step in range(0, n_ctx, 2):
        for mod_step in range(2):
            near = own if step + mod_step == 0 else from_plane(own, step, mod_step)
            parts[2 * step + mod_step] = near
            parts[2 * step + 2 + mod_step] = from_plane(near, 1, 0)
    made = sketches_of(parts, doc_lengths, n_ctx, n_mod, n_seq)
    sketch, shares = made[0], made[1:]
    gathered = [shares[0]] + [from_seq(shares[step], step) for step in range(1, n_seq)]
    ranks = proj_in.shape[0]
    row_pairs = ranks * ranks // LANES // n_ctx
    fisher = fisher_of(gathered, row_pairs, doc_lengths.shape[1] * n_seq)
    return (sketch, fisher)


def solution(mesh):
    placed = (
        P("seq", "ctx", "mod"),
        P("seq", "ctx", "mod"),
        P(None, "mod"),
        P(None, "mod"),
        P("seq", None),
    )
    return jax.shard_map(
        per_device,
        mesh=mesh,
        in_specs=placed,
        out_specs=(P("seq", ("ctx", "mod"), None), P("ctx", ("mod", "seq"))),
        check_vma=False,
    )
```
